32 devices in a mesh: tm: 8 (over y, x, core), group: 4 (over z).
Axes of the slice: x: 2, y: 2, z: 4, core: 2. Of those that a mesh axis runs over, the one named last changes fastest.
Arguments:
- propagators: float32 [8, 384, 384], P('tm'), may hold values from -1 to 1, as said below
- perturbation: float32 [8, 384, 384], P('tm', 'group'), as said below
Outputs:
- gradient: float32 [384, 384], P('tm')
The draws below stay inside these ranges and needn't reach their ends.
Inputs may be any that keep to these rules, and one draw needn't show every extreme that they name: `propagators`: each slice's matrix is orthogonal. `perturbation`: each slice's matrix is symmetric.
All inputs are finite; a program needn't handle non-finite values.
Results may differ from the reference program's by a relative error of at most 0.00028.
Values sent between devices are 32-bit elements; how exact they have to be, the bound alone decides.
No kernel may reach another device: no remote copies, remote signals or barrier semaphores. Data moves between devices by JAX's collectives and lax.ppermute only.
A program may use at most 128 MiB of HBM per device.

```python
import math
import jax
import jax.numpy as jnp
from jax import lax

D = 384
SLICES = 8


def draw_propagators(key, part):
    keys = jax.random.split(jax.random.fold_in(key, 11), SLICES)

    def single(one_key):
        raw = jax.random.normal(one_key, (D, D), jnp.float32)
        return jnp.linalg.qr(raw)[0]
    return jax.vmap(single)(keys)


def draw_perturbation(key, part):
    base_key = jax.random.fold_in(key, 7)
    raw = jax.random.normal(base_key, (SLICES, D, D), jnp.float32)
    return (raw + jnp.swapaxes(raw, 1, 2)) * (0.5 / math.sqrt(SLICES))


def setup_inputs(seed: int = 0) -> dict:
    streams_of = jax.random.split(jax.random.key(seed), 3)
    propagators = draw_propagators(jax.random.fold_in(streams_of[2], 71), 0)
    perturbation = draw_perturbation(jax.random.fold_in(streams_of[2], 71), 0)
    return {"propagators": propagators, "perturbation": perturbation}


def times_high(left, right):
    return jnp.dot(left.astype(jnp.float32), right.astype(jnp.float32), precision=lax.Precision.HIGHEST, preferred_element_type=jnp.float32)

def reference(propagators, perturbation):
    order_dim = propagators.shape[1]

    def advance(carry, pieces):
        before, total = carry
        propagator, symmetric = pieces
        pulled = times_high(symmetric, before)
        total = total + times_high(before.T, pulled)
        return ((times_high(propagator, before), total), None)
    start_carry = (jnp.eye(order_dim, dtype=jnp.float32), jnp.zeros((order_dim, order_dim), jnp.float32))
    (ending, gradient), unused = lax.scan(advance, start_carry, (propagators, perturbation))
    return gradient
```

```python
import jax
import jax.numpy as jnp
from jax import lax
from jax.sharding import PartitionSpec as P


def times(left, right):
    return lax.dot_general(left, right, (((1,), (0,)), ((), ())), precision=lax.Precision.HIGH, preferred_element_type=jnp.float32)


def times_t(left, right):
    return lax.dot_general(left, right, (((1,), (1,)), ((), ())), precision=lax.Precision.HIGH, preferred_element_type=jnp.float32)


def t_times(left, right):
    return lax.dot_general(left, right, (((0,), (0,)), ((), ())), precision=lax.Precision.HIGH, preferred_element_type=jnp.float32)


def body(propagators, perturbation):
    devices = lax.axis_size("tm")
    planes = lax.axis_size("group")
    chips = devices // 2
    order_dim = propagators.shape[1]
    block_rows = perturbation.shape[1]
    out_rows = order_dim // devices
    place = lax.axis_index("tm")
    plane = lax.axis_index("group")
    chip, core = place // 2, place % 2
    partner = [(i, i ^ 1) for i in range(devices)]

    own = propagators[0]
    other = lax.ppermute(own, "tm", partner)
    even = jnp.where(core == 0, own, other)
    odd = jnp.where(core == 0, other, own)

    rows = perturbation[0]
    full = jnp.zeros((order_dim, order_dim), jnp.float32)
    full = lax.dynamic_update_slice_in_dim(full, rows, plane * block_rows, 0)
    for shift in range(1, planes):
        got = lax.ppermute(rows, "group", [(i, (i + shift) % planes) for i in range(planes)])
        full = lax.dynamic_update_slice_in_dim(full, got, (plane - shift) % planes * block_rows, 0)

    pair = lax.dot_general(even, odd, (((0,), (1,)), ((), ())), precision=lax.Precision.HIGH, preferred_element_type=jnp.float32)

    def half_of(whole):
        split = whole.reshape(chips, 2, out_rows, order_dim)
        return lax.dynamic_index_in_dim(split, core, 1, False)

    half = half_of(pair)
    halves = []
    for shift in range(1, chips):
        halves.append(lax.ppermute(half, "tm", [(i, i + 2 * shift) for i in range(devices - 2 * shift)]))

    full_other = lax.ppermute(full, "tm", partner)
    full_even = jnp.where(core == 0, full, full_other)
    full_odd = jnp.where(core == 0, full_other, full)
    total = full_even + t_times(even, times(full_odd, even))

    identity = jnp.eye(order_dim, dtype=jnp.float32)
    for shift in range(1, chips):
        mine = halves[shift - 1]
        theirs = lax.ppermute(mine, "tm", partner)
        low = jnp.where(core == 0, mine, theirs)
        high = jnp.where(core == 0, theirs, mine)
        whole = jnp.stack([low, high], 1).reshape(order_dim, order_dim)
        whole = jnp.where(chip >= shift, whole, identity)
        if shift < chips - 1:
            total = times_t(times(whole, total), whole)
        else:
            left = jnp.where(chip >= shift, mine, half_of(identity)).reshape(order_dim // 2, order_dim)
            terms = times_t(times(left, total), whole).reshape(chips, out_rows, order_dim)
    out = lax.dynamic_index_in_dim(terms, chip, 0, False)
    for shift in range(1, chips):
        block = lax.dynamic_index_in_dim(terms, (chip + shift) % chips, 0, False)
        out = out + lax.ppermute(block, "tm", [(i, (i + 2 * shift) % devices) for i in range(devices)])
    return out


def solution(mesh):
    in_specs = (P("tm", None, None), P("tm", "group", None))
    out_specs = P("tm", None)
    return jax.shard_map(body, mesh=mesh, in_specs=in_specs, out_specs=out_specs, check_vma=False)
```

```python
import functools

import jax
import jax.numpy as jnp
from jax import lax
from jax.experimental import pallas as pl
from jax.experimental.pallas import tpu as pltpu
from jax.sharding import PartitionSpec as P

VMEM = pl.BlockSpec(memory_space=pltpu.VMEM)
F32, BF16 = jnp.float32, jnp.bfloat16


def product(left, right, left_dim, right_dim):
    dims = (((left_dim,), (right_dim,)), ((), ()))
    return lax.dot_general(left, right, dims, precision=lax.Precision.HIGH, preferred_element_type=F32)


def parts(x):
    high = x.astype(BF16)
    return high, (x - high.astype(F32)).astype(BF16)


def mul(left, right, right_dim=0):
    dims = (((1,), (right_dim,)), ((), ()))
    dot = functools.partial(lax.dot_general, dimension_numbers=dims, preferred_element_type=F32)
    return dot(left[0], right[0]) + (dot(left[0], right[1]) + dot(left[1], right[0]))


def call(kernel, outs, operands, scratch=(), flops=0):
    outs = tuple(jax.ShapeDtypeStruct(shape, F32) for shape in outs)
    return pl.pallas_call(
        kernel,
        out_shape=outs,
        in_specs=[VMEM] * len(operands),
        out_specs=(VMEM,) * len(outs),
        scratch_shapes=[pltpu.VMEM(shape, F32) for shape in scratch],
        cost_estimate=pl.CostEstimate(flops=flops, bytes_accessed=0, transcendentals=0),
        compiler_params=pltpu.CompilerParams(vmem_limit_bytes=12 * 2**20),
    )(*operands)


def pair_kernel(own, other, half, even_t, work):
    core = lax.rem(lax.axis_index("tm"), 2)
    chips, rows, order_dim = half.shape

    def run(even, odd):
        even_t[...] = even[...].T
        for k in range(chips):
            start = pl.multiple_of((2 * k + core) * rows, 8)
            work[k] = even_t[pl.ds(start, rows), :]
        left = parts(work[...].reshape(chips * rows, order_dim))
        half[...] = mul(left, parts(odd[...]), 1).reshape(half.shape)

    pl.when(core == 0)(lambda: run(own, other))
    pl.when(core == 1)(lambda: run(other, own))


def fill(whole, core, mine, theirs):
    whole[:, core] = mine[...]
    whole[:, 1 - core] = theirs[...]


def chain_kernel(chips, *refs):
    count = chips - 2
    mine, theirs, (out, whole) = refs[:count], refs[count : 2 * count], refs[2 * count :]
    place = lax.axis_index("tm")
    chip, core = place // 2, lax.rem(place, 2)
    order_dim = out.shape[0]
    for shift in range(1, chips - 1):

        @pl.when(chip > shift)
        def _(shift=shift):
            fill(whole, core, mine[shift - 1], theirs[shift - 1])
            step = whole[...].reshape(order_dim, order_dim)
            if shift == 1:
                out[...] = step
            else:
                out[...] = mul(parts(step), parts(out[...]))


def local_kernel(planes, *refs):
    mine, theirs = refs[:planes], refs[planes : 2 * planes]
    even_t, chain, out, both = refs[2 * planes :]
    place, plane = lax.axis_index("tm"), lax.axis_index("group")
    chip, core = place // 2, lax.rem(place, 2)
    rows = mine[0].shape[0]
    for shift in range(planes):
        start = pl.multiple_of(lax.rem(plane + planes - shift, planes) * rows, 8)
        both[core, pl.ds(start, rows), :] = mine[shift][...]
        both[1 - core, pl.ds(start, rows), :] = theirs[shift][...]
    left = parts(even_t[...])
    total = both[0] + mul(parts(mul(left, parts(both[1]))), left, 1)

    @pl.when(chip < 2)
    def _():
        out[...] = total

    @pl.when(chip >= 2)
    def _():
        left = parts(chain[...])
        out[...] = mul(parts(mul(left, parts(total))), left, 1)


def last_kernel(mine, theirs, total, out, whole):
    place = lax.axis_index("tm")
    chip, core = place // 2, lax.rem(place, 2)
    order_dim = total.shape[0]
    chips, rows = out.shape[:2]

    @pl.when(chip == 0)
    def _():
        for k in range(chips):
            out[k] = total[pl.ds(pl.multiple_of((2 * k + core) * rows, 8), rows), :]

    @pl.when(chip > 0)
    def _():
        fill(whole, core, mine, theirs)
        right = parts(whole[...].reshape(order_dim, order_dim))
        left = parts(mine[...].reshape(order_dim // 2, order_dim))
        out[...] = mul(parts(mul(left, parts(total[...]))), right, 1).reshape(out.shape)


def body(propagators, perturbation):
    devices = lax.axis_size("tm")
    planes = lax.axis_size("group")
    chips = devices // 2
    order_dim = propagators.shape[1]
    out_rows = order_dim // devices
    place = lax.axis_index("tm")
    chip = place // 2
    partner = [(i, i ^ 1) for i in range(devices)]
    swap = lambda x: lax.ppermute(x, "tm", partner)
    cube = 2 * order_dim**3

    def chip_pairs(pairs):
        return [(2 * i + c, 2 * j + c) for i, j in pairs for c in range(2)]

    own = propagators[0]
    rows = perturbation[0]
    other = swap(own)
    blocks = [rows]
    for shift in range(1, planes):
        blocks.append(lax.ppermute(rows, "group", [(i, (i + shift) % planes) for i in range(planes)]))
    half_shape = (chips, out_rows, order_dim)
    half, even_t = call(pair_kernel, [half_shape, own.shape], [own, other], [half_shape], 2 * cube)

    sent = []
    for shift in range(1, chips - 1):
        sent.append(lax.ppermute(half, "tm", chip_pairs([(i, i + shift) for i in range(1, chips - shift)])))
    first = []
    for shift in range(1, chips):
        first.append(lax.ppermute(half, "tm", chip_pairs([(0, shift)])))
    sent_other = []
    for shift in range(1, chips - 1):
        sent_other.append(swap(sent[shift - 1]))
    (chain,) = call(
        functools.partial(chain_kernel, chips), [own.shape], sent + sent_other,
        [(chips, 2, out_rows, order_dim)], 3 * cube,
    )
    blocks_other = []
    for shift in range(planes):
        blocks_other.append(swap(blocks[shift]))
    (total,) = call(
        functools.partial(local_kernel, planes), [own.shape],
        blocks + blocks_other + [even_t, chain], [(2,) + own.shape], 12 * cube,
    )
    mine = first[0]
    for shift in range(2, chips):
        mine = jnp.where(chip == shift, first[shift - 1], mine)
    theirs = swap(mine)
    (terms,) = call(last_kernel, [half_shape], [mine, theirs, total], [(chips, 2, out_rows, order_dim)], 3 * cube)
    out = lax.dynamic_index_in_dim(terms, chip, 0, False)
    for shift in range(chips - 1, 0, -1):
        block = lax.dynamic_index_in_dim(terms, chip ^ shift, 0, False)
        out = out + lax.ppermute(block, "tm", [(i, i ^ (2 * shift)) for i in range(devices)])
    return out


def plain_body(propagators, perturbation):
    devices = lax.axis_size("tm")
    planes = lax.axis_size("group")
    chips = devices // 2
    order_dim = propagators.shape[1]
    block_rows = perturbation.shape[1]
    out_rows = order_dim // devices
    place = lax.axis_index("tm")
    plane = lax.axis_index("group")
    chip, core = place // 2, place % 2
    partner = [(i, i ^ 1) for i in range(devices)]
    identity = jnp.eye(order_dim, dtype=F32)

    def half_of(whole):
        split = whole.reshape(chips, 2, out_rows, order_dim)
        return lax.dynamic_index_in_dim(split, core, 1, False)

    def by_core(mine, theirs):
        return jnp.where(core == 0, mine, theirs), jnp.where(core == 0, theirs, mine)

    own = propagators[0]
    even, odd = by_core(own, lax.ppermute(own, "tm", partner))
    rows = perturbation[0]
    full = jnp.zeros((order_dim, order_dim), F32)
    for shift in range(planes):
        got = rows
        if shift:
            got = lax.ppermute(rows, "group", [(i, (i + shift) % planes) for i in range(planes)])
        full = lax.dynamic_update_slice_in_dim(full, got, (plane - shift) % planes * block_rows, 0)
    half = half_of(product(even, odd, 0, 1))
    full_even, full_odd = by_core(full, lax.ppermute(full, "tm", partner))
    total = full_even + product(even, product(full_odd, even, 1, 0), 0, 0)
    for shift in range(1, chips):
        got = lax.ppermute(half, "tm", [(i, i + 2 * shift) for i in range(devices - 2 * shift)])
        mine = jnp.where(chip >= shift, got, half_of(identity))
        theirs = lax.ppermute(mine, "tm", partner)
        whole = jnp.stack(by_core(mine, theirs), 1).reshape(order_dim, order_dim)
        total = product(product(whole, total, 1, 0), whole, 1, 1)
    terms = half_of(total)
    out = lax.dynamic_index_in_dim(terms, chip, 0, False)
    for shift in range(1, chips):
        block = lax.dynamic_index_in_dim(terms, (chip + shift) % chips, 0, False)
        out = out + lax.ppermute(block, "tm", [(i, (i + 2 * shift) % devices) for i in range(devices)])
    return out


def solution(mesh):
    in_specs = (P("tm", None, None), P("tm", "group", None))
    out_specs = P("tm", None)
    chips, planes = mesh.shape["tm"] // 2, mesh.shape["group"]

    def step(propagators, perturbation):
        order_dim = propagators.shape[1]
        tiled = order_dim // planes % 8 == 0 and order_dim // (2 * chips) % 8 == 0
        power = chips & (chips - 1) == 0 and chips > 2
        plan = body if tiled and power else plain_body
        return jax.shard_map(plan, mesh=mesh, in_specs=in_specs, out_specs=out_specs, check_vma=False)(
            propagators, perturbation
        )

    return step
```

```python
import functools

import jax
import jax.numpy as jnp
from jax import lax
from jax.experimental import pallas as pl
from jax.experimental.pallas import tpu as pltpu
from jax.sharding import PartitionSpec as P

VMEM = pl.BlockSpec(memory_space=pltpu.VMEM)
F32, BF16 = jnp.float32, jnp.bfloat16


def product(left, right, left_dim, right_dim):
    dims = (((left_dim,), (right_dim,)), ((), ()))
    return lax.dot_general(left, right, dims, precision=lax.Precision.HIGH, preferred_element_type=F32)


def parts(x):
    high = x.astype(BF16)
    return high, (x - high.astype(F32)).astype(BF16)


def mul(left, right, right_dim=0):
    dims = (((1,), (right_dim,)), ((), ()))
    lefts = jnp.concatenate([left[0], left[1], left[0]], 1)
    rights = jnp.concatenate([right[0], right[0], right[1]], right_dim)
    return lax.dot_general(lefts, rights, dims, preferred_element_type=F32)


def call(kernel, outs, operands, scratch=(), flops=0):
    outs = tuple(jax.ShapeDtypeStruct(shape, F32) for shape in outs)
    return pl.pallas_call(
        kernel,
        out_shape=outs,
        in_specs=[VMEM] * len(operands),
        out_specs=(VMEM,) * len(outs),
        scratch_shapes=[pltpu.VMEM(shape, F32) for shape in scratch],
        cost_estimate=pl.CostEstimate(flops=flops, bytes_accessed=0, transcendentals=0),
        compiler_params=pltpu.CompilerParams(vmem_limit_bytes=12 * 2**20),
    )(*operands)


def load_kernel(own, copy):
    copy[...] = own[...]


def pair_kernel(own, other, half, even_t, work):
    core = lax.rem(lax.axis_index("tm"), 2)
    chips, rows, order_dim = half.shape

    def run(even, odd):
        even_t[...] = even[...].T
        for k in range(chips):
            start = pl.multiple_of((2 * k + core) * rows, 8)
            work[k] = even_t[pl.ds(start, rows), :]
        left = parts(work[...].reshape(chips * rows, order_dim))
        half[...] = mul(left, parts(odd[...]), 1).reshape(half.shape)

    pl.when(core == 0)(lambda: run(own, other))
    pl.when(core == 1)(lambda: run(other, own))


def fill(whole, core, mine, theirs):
    whole[:, core] = mine[...]
    whole[:, 1 - core] = theirs[...]


def chain_kernel(near, near_other, across, across_other, out, whole):
    place = lax.axis_index("tm")
    chip, core = place // 2, lax.rem(place, 2)

    @pl.when(chip == 3)
    def _():
        fill(whole, core, across, across_other)
        left = parts(whole[...].reshape(out.shape))
        fill(whole, core, near, near_other)
        out[...] = mul(left, parts(whole[...].reshape(out.shape)))


def local_kernel(planes, *refs):
    mine, theirs = refs[:planes], refs[planes : 2 * planes]
    even_t, chain, out, both = refs[2 * planes :]
    place, plane = lax.axis_index("tm"), lax.axis_index("group")
    chip, core = place // 2, lax.rem(place, 2)
    rows = mine[0].shape[0]
    for shift in range(planes):
        start = pl.multiple_of(lax.rem(plane + planes - shift, planes) * rows, 8)
        both[core, pl.ds(start, rows), :] = mine[shift][...]
        both[1 - core, pl.ds(start, rows), :] = theirs[shift][...]
    left = parts(even_t[...])
    total = both[0] + mul(parts(mul(left, parts(both[1]))), left, 1)

    @pl.when(chip < 3)
    def _():
        out[...] = total

    @pl.when(chip == 3)
    def _():
        left = parts(chain[...])
        out[...] = mul(parts(mul(left, parts(total))), left, 1)


def left_kernel(near, far, total, out):
    place = lax.axis_index("tm")
    chip, core = place // 2, lax.rem(place, 2)
    chips, rows, order_dim = out.shape

    @pl.when(chip == 0)
    def _():
        for k in range(chips):
            out[k] = total[pl.ds(pl.multiple_of((2 * k + core) * rows, 8), rows), :]

    def run(mine):
        left = parts(mine[...].reshape(chips * rows, order_dim))
        out[...] = mul(left, parts(total[...])).reshape(out.shape)

    pl.when(chip == 1)(lambda: run(near))
    pl.when(chip == 3)(lambda: run(far))


def right_kernel(near, near_other, across, across_other, far, far_other, left, total, out, whole):
    place = lax.axis_index("tm")
    chip, core = place // 2, lax.rem(place, 2)
    chips, rows, order_dim = out.shape
    tall, square = (chips * rows, order_dim), total.shape

    @pl.when(chip == 0)
    def _():
        out[...] = left[...]

    def run(mine, theirs):
        fill(whole, core, mine, theirs)
        right = parts(whole[...].reshape(square))
        out[...] = mul(parts(left[...].reshape(tall)), right, 1).reshape(out.shape)

    pl.when(chip == 1)(lambda: run(near, near_other))
    pl.when(chip == 3)(lambda: run(far, far_other))

    @pl.when(chip == 2)
    def _():
        fill(whole, core, far, far_other)
        right = parts(whole[...].reshape(square))
        value = mul(parts(across[...].reshape(tall)), right)
        value = mul(parts(mul(parts(value), parts(total[...]))), right, 1)
        fill(whole, core, across, across_other)
        right = parts(whole[...].reshape(square))
        out[...] = mul(parts(value), right, 1).reshape(out.shape)


def body(propagators, perturbation):
    devices = lax.axis_size("tm")
    planes = lax.axis_size("group")
    chips = devices // 2
    order_dim = propagators.shape[1]
    out_rows = order_dim // devices
    chip = lax.axis_index("tm") // 2
    swap = lambda x: lax.ppermute(x, "tm", [(i, i ^ 1) for i in range(devices)])
    cube = 2 * order_dim**3
    half_shape = (chips, out_rows, order_dim)
    whole_shape = (chips, 2, out_rows, order_dim)

    own = propagators[0]
    rows = perturbation[0]
    other = swap(own)
    blocks = [rows]
    for shift in range(1, planes):
        blocks.append(lax.ppermute(rows, "group", [(i, (i + shift) % planes) for i in range(planes)]))
    (own,) = call(load_kernel, [own.shape], [own])
    half, even_t = call(pair_kernel, [half_shape, own.shape], [own, other], [half_shape], 2 * cube)

    mine, theirs = {}, {}
    for way in (2, 1, 3):
        pairs = [(i, i ^ (2 * way)) for i in range(devices) if i < i ^ (2 * way)]
        mine[way] = lax.ppermute(half, "tm", pairs)
    for way in (2, 1, 3):
        theirs[way] = swap(mine[way])
    operands = [mine[1], theirs[1], mine[2], theirs[2]]
    (chain,) = call(chain_kernel, [own.shape], operands, [whole_shape], 2 * cube)
    blocks_other = []
    for shift in range(planes):
        blocks_other.append(swap(blocks[shift]))
    operands = blocks + blocks_other + [even_t, chain]
    kernel = functools.partial(local_kernel, planes)
    (total,) = call(kernel, [own.shape], operands, [(2,) + own.shape], 12 * cube)
    (left,) = call(left_kernel, [half_shape], [mine[1], mine[3], total], [], 2 * cube)
    operands = [x[way] for way in (1, 2, 3) for x in (mine, theirs)] + [left, total]
    (terms,) = call(right_kernel, [half_shape], operands, [whole_shape], 2 * cube)
    out = lax.dynamic_index_in_dim(terms, chip, 0, False)
    for way in (3, 2, 1):
        block = lax.dynamic_index_in_dim(terms, chip ^ way, 0, False)
        out = out + lax.ppermute(block, "tm", [(i, i ^ (2 * way)) for i in range(devices)])
    return out


def plain_body(propagators, perturbation):
    devices = lax.axis_size("tm")
    planes = lax.axis_size("group")
    chips = devices // 2
    order_dim = propagators.shape[1]
    block_rows = perturbation.shape[1]
    out_rows = order_dim // devices
    place = lax.axis_index("tm")
    plane = lax.axis_index("group")
    chip, core = place // 2, place % 2
    partner = [(i, i ^ 1) for i in range(devices)]
    identity = jnp.eye(order_dim, dtype=F32)

    def half_of(whole):
        split = whole.reshape(chips, 2, out_rows, order_dim)
        return lax.dynamic_index_in_dim(split, core, 1, False)

    def by_core(mine, theirs):
        return jnp.where(core == 0, mine, theirs), jnp.where(core == 0, theirs, mine)

    own = propagators[0]
    even, odd = by_core(own, lax.ppermute(own, "tm", partner))
    rows = perturbation[0]
    full = jnp.zeros((order_dim, order_dim), F32)
    for shift in range(planes):
        got = rows
        if shift:
            got = lax.ppermute(rows, "group", [(i, (i + shift) % planes) for i in range(planes)])
        full = lax.dynamic_update_slice_in_dim(full, got, (plane - shift) % planes * block_rows, 0)
    half = half_of(product(even, odd, 0, 1))
    full_even, full_odd = by_core(full, lax.ppermute(full, "tm", partner))
    total = full_even + product(even, product(full_odd, even, 1, 0), 0, 0)
    for shift in range(1, chips):
        got = lax.ppermute(half, "tm", [(i, i + 2 * shift) for i in range(devices - 2 * shift)])
        mine = jnp.where(chip >= shift, got, half_of(identity))
        theirs = lax.ppermute(mine, "tm", partner)
        whole = jnp.stack(by_core(mine, theirs), 1).reshape(order_dim, order_dim)
        total = product(product(whole, total, 1, 0), whole, 1, 1)
    terms = half_of(total)
    out = lax.dynamic_index_in_dim(terms, chip, 0, False)
    for shift in range(1, chips):
        block = lax.dynamic_index_in_dim(terms, (chip + shift) % chips, 0, False)
        out = out + lax.ppermute(block, "tm", [(i, (i + 2 * shift) % devices) for i in range(devices)])
    return out


def solution(mesh):
    in_specs = (P("tm", None, None), P("tm", "group", None))
    out_specs = P("tm", None)
    chips, planes = mesh.shape["tm"] // 2, mesh.shape["group"]

    def step(propagators, perturbation):
        order_dim = propagators.shape[1]
        tiled = order_dim // planes % 8 == 0 and order_dim // (2 * chips) % 8 == 0
        plan = body if tiled and chips == 4 else plain_body
        return jax.shard_map(plan, mesh=mesh, in_specs=in_specs, out_specs=out_specs, check_vma=False)(
            propagators, perturbation
        )

    return step
```

```python
import jax
import jax.numpy as jnp
from jax import lax
from jax.experimental import pallas as pl
from jax.experimental.pallas import tpu as pltpu
from jax.sharding import PartitionSpec as P

VMEM = pl.BlockSpec(memory_space=pltpu.VMEM)
F32, BF16 = jnp.float32, jnp.bfloat16


def product(left, right, left_dim, right_dim):
    dims = (((left_dim,), (right_dim,)), ((), ()))
    return lax.dot_general(left, right, dims, precision=lax.Precision.HIGH, preferred_element_type=F32)


def parts(x):
    high = x.astype(BF16)
    return high, (x - high.astype(F32)).astype(BF16)


def mul(left, right, right_dim=0):
    dims = (((1,), (right_dim,)), ((), ()))
    lefts = jnp.concatenate([left[0], left[1], left[0]], 1)
    rights = jnp.concatenate([right[0], right[0], right[1]], right_dim)
    return lax.dot_general(lefts, rights, dims, preferred_element_type=F32)


def call(kernel, outs, operands, scratch=(), flops=0):
    outs = tuple(jax.ShapeDtypeStruct(shape, F32) for shape in outs)
    return pl.pallas_call(
        kernel,
        out_shape=outs,
        in_specs=[VMEM] * len(operands),
        out_specs=(VMEM,) * len(outs),
        scratch_shapes=[pltpu.VMEM(shape, F32) for shape in scratch],
        cost_estimate=pl.CostEstimate(flops=flops, bytes_accessed=0, transcendentals=0),
        compiler_params=pltpu.CompilerParams(vmem_limit_bytes=12 * 2**20),
    )(*operands)


def load_kernel(own, rows, copy, part):
    plane = lax.axis_index("group")
    lanes = part.shape[1]
    copy[...] = own[...]

    @pl.when(plane < 2)
    def _():
        part[...] = rows[:, :lanes]

    @pl.when(plane >= 2)
    def _():
        part[...] = rows[:, lanes // 2 :]


def pair_kernel(own, other, half, even_t, work):
    core = lax.rem(lax.axis_index("tm"), 2)
    chips, rows, order_dim = half.shape

    def run(even, odd):
        even_t[...] = even[...].T
        for k in range(chips):
            start = pl.multiple_of((2 * k + core) * rows, 8)
            work[k] = even_t[pl.ds(start, rows), :]
        left = parts(work[...].reshape(chips * rows, order_dim))
        half[...] = mul(left, parts(odd[...]), 1).reshape(half.shape)

    pl.when(core == 0)(lambda: run(own, other))
    pl.when(core == 1)(lambda: run(other, own))


def fill(whole, core, mine, theirs):
    whole[:, core] = mine[...]
    whole[:, 1 - core] = theirs[...]


def carry_kernel(even_t, step, step_other, skip, skip_other, out, whole):
    place = lax.axis_index("tm")
    chip, core = place // 2, lax.rem(place, 2)
    shape = out.shape

    @pl.when((chip < 2) & (core == 1))
    def _():
        out[...] = even_t[...]

    @pl.when(chip >= 2)
    def _():
        fill(whole, core, step, step_other)
        out[...] = whole[...].reshape(shape)

    @pl.when(chip == 3)
    def _():
        fill(whole, core, skip, skip_other)
        out[...] = mul(parts(whole[...].reshape(shape)), parts(out[...]))

    @pl.when((chip >= 2) & (core == 1))
    def _():
        out[...] = mul(parts(out[...]), parts(even_t[...]))


def local_kernel(rows, beside, skip, cross, carry, out, full):
    place, plane = lax.axis_index("tm"), lax.axis_index("group")
    chip, core = place // 2, lax.rem(place, 2)
    count, lanes = rows.shape[0], skip.shape[1]
    next_to = plane + 1 - 2 * lax.rem(plane, 2)

    def at(block):
        return pl.ds(pl.multiple_of(block * count, 8), count)

    full[at(plane), :] = rows[...]
    full[at(next_to), :] = beside[...]

    @pl.when(plane < 2)
    def _():
        full[at(plane + 2), lanes // 2 :] = skip[...]
        full[at(3 - plane), lanes // 2 :] = cross[...]

    @pl.when(plane >= 2)
    def _():
        full[at(plane - 2), :lanes] = skip[...]
        full[at(3 - plane), :lanes] = cross[...]

    row = lax.broadcasted_iota(jnp.int32, full.shape, 0)
    lane = lax.broadcasted_iota(jnp.int32, full.shape, 1)
    low = (row < 2 * count) & (lane < jnp.where(plane < 2, 2 * lanes, lanes))
    high = (row >= 2 * count) & (lane >= jnp.where(plane < 2, lanes // 2, 0))
    value = jnp.where(low | high, full[...], full[...].T)
    plain = (chip < 2) & (core == 0)

    @pl.when(plain)
    def _():
        out[...] = value

    @pl.when(jnp.logical_not(plain))
    def _():
        left = parts(carry[...])
        out[...] = mul(parts(mul(left, parts(value))), left, 1)


def pick_kernel(first, second, third, out):
    chip = lax.axis_index("tm") // 2
    for k, half in ((1, first), (2, second), (3, third)):

        @pl.when(chip == k)
        def _(half=half):
            out[...] = half[...]


def left_kernel(mine, one, two, out, total):
    place = lax.axis_index("tm")
    chip, core = place // 2, lax.rem(place, 2)
    chips, rows, order_dim = out.shape
    total[...] = one[...] + two[...]

    @pl.when(chip == 0)
    def _():
        for k in range(chips):
            out[k] = total[pl.ds(pl.multiple_of((2 * k + core) * rows, 8), rows), :]

    @pl.when(chip > 0)
    def _():
        left = parts(mine[...].reshape(chips * rows, order_dim))
        out[...] = mul(left, parts(total[...])).reshape(out.shape)


def right_kernel(mine, theirs, left, out, whole):
    place = lax.axis_index("tm")
    chip, core = place // 2, lax.rem(place, 2)
    chips, rows, order_dim = out.shape

    @pl.when(chip == 0)
    def _():
        out[...] = left[...]

    @pl.when(chip > 0)
    def _():
        fill(whole, core, mine, theirs)
        right = parts(whole[...].reshape(order_dim, order_dim))
        out[...] = mul(parts(left[...].reshape(chips * rows, order_dim)), right, 1).reshape(out.shape)


def body(propagators, perturbation):
    devices = lax.axis_size("tm")
    planes = lax.axis_size("group")
    chips = devices // 2
    order_dim = propagators.shape[1]
    out_rows = order_dim // devices
    chip = lax.axis_index("tm") // 2
    swap = lambda x: lax.ppermute(x, "tm", [(i, i ^ 1) for i in range(devices)])
    cube = 2 * order_dim**3
    block_rows = perturbation.shape[1]
    half_shape = (chips, out_rows, order_dim)
    whole_shape = (chips, 2, out_rows, order_dim)

    own = propagators[0]
    rows = perturbation[0]
    other = swap(own)
    own, part = call(load_kernel, [own.shape, (block_rows, order_dim // 3 * 2)], [own, rows])
    near = {}
    for name, sent, way in (("beside", rows, 1), ("skip", part, 2), ("cross", part, 3)):
        near[name] = lax.ppermute(sent, "group", [(i, i ^ way) for i in range(planes)])
    half, even_t = call(pair_kernel, [half_shape, own.shape], [own, other], [half_shape], 2 * cube)

    routes = {"skip": [(1, 3)], "step": [(0, 1), (1, 2), (2, 3)], "far": [(0, 3)], "across": [(0, 2)]}
    got, other = {}, {}
    for name, links in routes.items():
        got[name] = lax.ppermute(half, "tm", [(2 * i + c, 2 * j + c) for i, j in links for c in range(2)])
    for name in ("skip", "step"):
        other[name] = swap(got[name])
    operands = [even_t] + [x[name] for name in ("step", "skip") for x in (got, other)]
    (carry,) = call(carry_kernel, [own.shape], operands, [whole_shape], 2 * cube)
    operands = [rows] + [near[name] for name in ("beside", "skip", "cross")] + [carry]
    (one,) = call(local_kernel, [own.shape], operands, [own.shape], 6 * cube)
    two = swap(one)
    (mine,) = call(pick_kernel, [half_shape], [got[name] for name in ("step", "across", "far")])
    theirs = swap(mine)
    (left,) = call(left_kernel, [half_shape], [mine, one, two], [own.shape], 2 * cube)
    (terms,) = call(right_kernel, [half_shape], [mine, theirs, left], [whole_shape], 2 * cube)
    out = lax.dynamic_index_in_dim(terms, chip, 0, False)
    for way in (3, 2, 1):
        block = lax.dynamic_index_in_dim(terms, chip ^ way, 0, False)
        out = out + lax.ppermute(block, "tm", [(i, i ^ (2 * way)) for i in range(devices)])
    return out


def plain_body(propagators, perturbation):
    devices = lax.axis_size("tm")
    planes = lax.axis_size("group")
    chips = devices // 2
    order_dim = propagators.shape[1]
    block_rows = perturbation.shape[1]
    out_rows = order_dim // devices
    place = lax.axis_index("tm")
    plane = lax.axis_index("group")
    chip, core = place // 2, place % 2
    partner = [(i, i ^ 1) for i in range(devices)]
    identity = jnp.eye(order_dim, dtype=F32)

    def half_of(whole):
        split = whole.reshape(chips, 2, out_rows, order_dim)
        return lax.dynamic_index_in_dim(split, core, 1, False)

    def by_core(mine, theirs):
        return jnp.where(core == 0, mine, theirs), jnp.where(core == 0, theirs, mine)

    own = propagators[0]
    even, odd = by_core(own, lax.ppermute(own, "tm", partner))
    rows = perturbation[0]
    full = jnp.zeros((order_dim, order_dim), F32)
    for shift in range(planes):
        got = rows
        if shift:
            got = lax.ppermute(rows, "group", [(i, (i + shift) % planes) for i in range(planes)])
        full = lax.dynamic_update_slice_in_dim(full, got, (plane - shift) % planes * block_rows, 0)
    half = half_of(product(even, odd, 0, 1))
    full_even, full_odd = by_core(full, lax.ppermute(full, "tm", partner))
    total = full_even + product(even, product(full_odd, even, 1, 0), 0, 0)
    for shift in range(1, chips):
        got = lax.ppermute(half, "tm", [(i, i + 2 * shift) for i in range(devices - 2 * shift)])
        mine = jnp.where(chip >= shift, got, half_of(identity))
        theirs = lax.ppermute(mine, "tm", partner)
        whole = jnp.stack(by_core(mine, theirs), 1).reshape(order_dim, order_dim)
        total = product(product(whole, total, 1, 0), whole, 1, 1)
    terms = half_of(total)
    out = lax.dynamic_index_in_dim(terms, chip, 0, False)
    for shift in range(1, chips):
        block = lax.dynamic_index_in_dim(terms, (chip + shift) % chips, 0, False)
        out = out + lax.ppermute(block, "tm", [(i, (i + 2 * shift) % devices) for i in range(devices)])
    return out


def solution(mesh):
    in_specs = (P("tm", None, None), P("tm", "group", None))
    out_specs = P("tm", None)
    chips, planes = mesh.shape["tm"] // 2, mesh.shape["group"]

    def step(propagators, perturbation):
        order_dim = propagators.shape[1]
        tiled = order_dim // planes % 8 == 0 and order_dim // (2 * chips) % 8 == 0 and order_dim % 384 == 0
        plan = body if tiled and chips == 4 and planes == 4 else plain_body
        return jax.shard_map(plan, mesh=mesh, in_specs=in_specs, out_specs=out_specs, check_vma=False)(
            propagators, perturbation
        )

    return step
```

```python
import jax
import jax.numpy as jnp
from jax import lax
from jax.experimental import pallas as pl
from jax.experimental.pallas import tpu as pltpu
from jax.sharding import PartitionSpec as P

VMEM = pl.BlockSpec(memory_space=pltpu.VMEM)
F32, BF16 = jnp.float32, jnp.bfloat16


def product(left, right, left_dim, right_dim):
    dims = (((left_dim,), (right_dim,)), ((), ()))
    return lax.dot_general(left, right, dims, precision=lax.Precision.HIGH, preferred_element_type=F32)


def parts(x):
    high = x.astype(BF16)
    return high, (x - high.astype(F32)).astype(BF16)


def mul(left, right, right_dim=0):
    dims = (((1,), (right_dim,)), ((), ()))
    lefts = jnp.concatenate([left[0], left[1], left[0]], 1)
    rights = jnp.concatenate([right[0], right[0], right[1]], right_dim)
    return lax.dot_general(lefts, rights, dims, preferred_element_type=F32)


def call(kernel, outs, operands, scratch=(), flops=0):
    outs = tuple(jax.ShapeDtypeStruct(shape, F32) for shape in outs)
    return pl.pallas_call(
        kernel,
        out_shape=outs,
        in_specs=[VMEM] * len(operands),
        out_specs=(VMEM,) * len(outs),
        scratch_shapes=[pltpu.VMEM(shape, F32) for shape in scratch],
        cost_estimate=pl.CostEstimate(flops=flops, bytes_accessed=0, transcendentals=0),
        compiler_params=pltpu.CompilerParams(vmem_limit_bytes=12 * 2**20),
    )(*operands)


def load_kernel(own, rows, copy, rows_copy, part):
    plane = lax.axis_index("group")
    lanes = part.shape[1]
    copy[...] = own[...]
    rows_copy[...] = rows[...]

    @pl.when(plane < 2)
    def _():
        part[...] = rows[:, :lanes]

    @pl.when(plane >= 2)
    def _():
        part[...] = rows[:, lanes // 2 :]


def pair_kernel(own, other, half, even_t, work):
    place = lax.axis_index("tm")
    chip, core = place // 2, lax.rem(place, 2)
    chips, rows, order_dim = half.shape
    used = chip < chips - 1

    def run(even, odd):
        even_t[...] = even[...].T
        for k in range(chips):
            start = pl.multiple_of((2 * k + core) * rows, 8)
            work[k] = even_t[pl.ds(start, rows), :]
        left = parts(work[...].reshape(chips * rows, order_dim))
        half[...] = mul(left, parts(odd[...]), 1).reshape(half.shape)

    pl.when(used & (core == 0))(lambda: run(own, other))
    pl.when(used & (core == 1))(lambda: run(other, own))


def fill(whole, core, mine, theirs):
    whole[:, core] = mine[...]
    whole[:, 1 - core] = theirs[...]


def carry_kernel(even_t, even, step, step_other, skip, skip_other, out, whole):
    place = lax.axis_index("tm")
    chip, core = place // 2, lax.rem(place, 2)
    shape = out.shape

    @pl.when((chip < 2) & (core == 1))
    def _():
        out[...] = even_t[...]

    @pl.when(chip >= 2)
    def _():
        fill(whole, core, step, step_other)
        out[...] = whole[...].reshape(shape)

    @pl.when(chip == 3)
    def _():
        fill(whole, core, skip, skip_other)
        out[...] = mul(parts(whole[...].reshape(shape)), parts(out[...]))

    @pl.when((chip == 2) & (core == 1))
    def _():
        out[...] = mul(parts(out[...]), parts(even_t[...]))

    @pl.when((chip == 3) & (core == 1))
    def _():
        out[...] = mul(parts(out[...]), parts(even[...]), 1)


def local_kernel(rows, beside, skip, cross, carry, out, full):
    place, plane = lax.axis_index("tm"), lax.axis_index("group")
    chip, core = place // 2, lax.rem(place, 2)
    count, lanes = rows.shape[0], skip.shape[1]
    next_to = plane + 1 - 2 * lax.rem(plane, 2)

    def at(block):
        return pl.ds(pl.multiple_of(block * count, 8), count)

    full[at(plane), :] = rows[...]
    full[at(next_to), :] = beside[...]

    @pl.when(plane < 2)
    def _():
        full[at(plane + 2), lanes // 2 :] = skip[...]
        full[at(3 - plane), lanes // 2 :] = cross[...]

    @pl.when(plane >= 2)
    def _():
        full[at(plane - 2), :lanes] = skip[...]
        full[at(3 - plane), :lanes] = cross[...]

    row = lax.broadcasted_iota(jnp.int32, full.shape, 0)
    lane = lax.broadcasted_iota(jnp.int32, full.shape, 1)
    low = (row < 2 * count) & (lane < jnp.where(plane < 2, 2 * lanes, lanes))
    high = (row >= 2 * count) & (lane >= jnp.where(plane < 2, lanes // 2, 0))
    value = jnp.where(low | high, full[...], full[...].T)
    plain = (chip < 2) & (core == 0)

    @pl.when(plain)
    def _():
        out[...] = value

    @pl.when(jnp.logical_not(plain))
    def _():
        left = parts(carry[...])
        out[...] = mul(parts(mul(left, parts(value))), left, 1)


def pick_kernel(first, second, third, out):
    chip = lax.axis_index("tm") // 2
    for k, half in ((1, first), (2, second), (3, third)):

        @pl.when(chip == k)
        def _(half=half):
            out[...] = half[...]


def left_kernel(mine, one, two, out, total):
    place = lax.axis_index("tm")
    chip, core = place // 2, lax.rem(place, 2)
    chips, rows, order_dim = out.shape
    total[...] = one[...] + two[...]

    @pl.when(chip == 0)
    def _():
        for k in range(chips):
            out[k] = total[pl.ds(pl.multiple_of((2 * k + core) * rows, 8), rows), :]

    @pl.when(chip > 0)
    def _():
        left = parts(mine[...].reshape(chips * rows, order_dim))
        out[...] = mul(left, parts(total[...])).reshape(out.shape)


def right_kernel(mine, theirs, left, out, whole):
    place = lax.axis_index("tm")
    chip, core = place // 2, lax.rem(place, 2)
    chips, rows, order_dim = out.shape

    @pl.when(chip == 0)
    def _():
        out[...] = left[...]

    @pl.when(chip > 0)
    def _():
        fill(whole, core, mine, theirs)
        right = parts(whole[...].reshape(order_dim, order_dim))
        out[...] = mul(parts(left[...].reshape(chips * rows, order_dim)), right, 1).reshape(out.shape)


def body(propagators, perturbation):
    devices = lax.axis_size("tm")
    planes = lax.axis_size("group")
    chips = devices // 2
    order_dim = propagators.shape[1]
    out_rows = order_dim // devices
    chip = lax.axis_index("tm") // 2
    swap = lambda x: lax.ppermute(x, "tm", [(i, i ^ 1) for i in range(devices)])
    cube = 2 * order_dim**3
    block_rows = perturbation.shape[1]
    half_shape = (chips, out_rows, order_dim)
    whole_shape = (chips, 2, out_rows, order_dim)

    own = propagators[0]
    rows = perturbation[0]
    other = swap(own)
    shapes = [own.shape, rows.shape, (block_rows, order_dim // 3 * 2)]
    own, rows, part = call(load_kernel, shapes, [own, rows])
    near = {}
    for name, sent, way in (("beside", rows, 1), ("skip", part, 2), ("cross", part, 3)):
        near[name] = lax.ppermute(sent, "group", [(i, i ^ way) for i in range(planes)])
    half, even_t = call(pair_kernel, [half_shape, own.shape], [own, other], [half_shape], 2 * cube)

    routes = {"skip": [(1, 3)], "step": [(0, 1), (1, 2), (2, 3)], "far": [(0, 3)], "across": [(0, 2)]}
    got, paired = {}, {}
    for name, links in routes.items():
        got[name] = lax.ppermute(half, "tm", [(2 * i + c, 2 * j + c) for i, j in links for c in range(2)])
    for name in ("skip", "step"):
        paired[name] = swap(got[name])
    operands = [even_t, other] + [x[name] for name in ("step", "skip") for x in (got, paired)]
    (carry,) = call(carry_kernel, [own.shape], operands, [whole_shape], 2 * cube)
    operands = [rows] + [near[name] for name in ("beside", "skip", "cross")] + [carry]
    (one,) = call(local_kernel, [own.shape], operands, [own.shape], 6 * cube)
    two = swap(one)
    (mine,) = call(pick_kernel, [half_shape], [got[name] for name in ("step", "across", "far")])
    theirs = swap(mine)
    (left,) = call(left_kernel, [half_shape], [mine, one, two], [own.shape], 2 * cube)
    (terms,) = call(right_kernel, [half_shape], [mine, theirs, left], [whole_shape], 2 * cube)
    out = lax.dynamic_index_in_dim(terms, chip, 0, False)
    for way in (3, 2, 1):
        block = lax.dynamic_index_in_dim(terms, chip ^ way, 0, False)
        out = out + lax.ppermute(block, "tm", [(i, i ^ (2 * way)) for i in range(devices)])
    return out


def plain_body(propagators, perturbation):
    devices = lax.axis_size("tm")
    planes = lax.axis_size("group")
    chips = devices // 2
    order_dim = propagators.shape[1]
    block_rows = perturbation.shape[1]
    out_rows = order_dim // devices
    place = lax.axis_index("tm")
    plane = lax.axis_index("group")
    chip, core = place // 2, place % 2
    partner = [(i, i ^ 1) for i in range(devices)]
    identity = jnp.eye(order_dim, dtype=F32)

    def half_of(whole):
        split = whole.reshape(chips, 2, out_rows, order_dim)
        return lax.dynamic_index_in_dim(split, core, 1, False)

    def by_core(mine, theirs):
        return jnp.where(core == 0, mine, theirs), jnp.where(core == 0, theirs, mine)

    own = propagators[0]
    even, odd = by_core(own, lax.ppermute(own, "tm", partner))
    rows = perturbation[0]
    full = jnp.zeros((order_dim, order_dim), F32)
    for shift in range(planes):
        got = rows
        if shift:
            got = lax.ppermute(rows, "group", [(i, (i + shift) % planes) for i in range(planes)])
        full = lax.dynamic_update_slice_in_dim(full, got, (plane - shift) % planes * block_rows, 0)
    half = half_of(product(even, odd, 0, 1))
    full_even, full_odd = by_core(full, lax.ppermute(full, "tm", partner))
    total = full_even + product(even, product(full_odd, even, 1, 0), 0, 0)
    for shift in range(1, chips):
        got = lax.ppermute(half, "tm", [(i, i + 2 * shift) for i in range(devices - 2 * shift)])
        mine = jnp.where(chip >= shift, got, half_of(identity))
        theirs = lax.ppermute(mine, "tm", partner)
        whole = jnp.stack(by_core(mine, theirs), 1).reshape(order_dim, order_dim)
        total = product(product(whole, total, 1, 0), whole, 1, 1)
    terms = half_of(total)
    out = lax.dynamic_index_in_dim(terms, chip, 0, False)
    for shift in range(1, chips):
        block = lax.dynamic_index_in_dim(terms, (chip + shift) % chips, 0, False)
        out = out + lax.ppermute(block, "tm", [(i, (i + 2 * shift) % devices) for i in range(devices)])
    return out


def solution(mesh):
    in_specs = (P("tm", None, None), P("tm", "group", None))
    out_specs = P("tm", None)
    chips, planes = mesh.shape["tm"] // 2, mesh.shape["group"]

    def step(propagators, perturbation):
        order_dim = propagators.shape[1]
        tiled = order_dim // planes % 8 == 0 and order_dim // (2 * chips) % 8 == 0 and order_dim % 384 == 0
        plan = body if tiled and chips == 4 and planes == 4 else plain_body
        return jax.shard_map(plan, mesh=mesh, in_specs=in_specs, out_specs=out_specs, check_vma=False)(
            propagators, perturbation
        )

    return step
```

```python
import jax
import jax.numpy as jnp
from jax import lax
from jax.experimental import pallas as pl
from jax.experimental.pallas import tpu as pltpu
from jax.sharding import PartitionSpec as P

VMEM = pl.BlockSpec(memory_space=pltpu.VMEM)
F32, BF16 = jnp.float32, jnp.bfloat16


def product(left, right, left_dim, right_dim):
    dims = (((left_dim,), (right_dim,)), ((), ()))
    return lax.dot_general(left, right, dims, precision=lax.Precision.HIGH, preferred_element_type=F32)


def parts(x):
    high = x.astype(BF16)
    return high, (x - high.astype(F32)).astype(BF16)


def mul(left, right, right_dim=0):
    dims = (((1,), (right_dim,)), ((), ()))
    lefts = jnp.concatenate([left[0], left[1], left[0]], 1)
    rights = jnp.concatenate([right[0], right[0], right[1]], right_dim)
    return lax.dot_general(lefts, rights, dims, preferred_element_type=F32)


def call(kernel, outs, operands, scratch=(), flops=0):
    outs = tuple(jax.ShapeDtypeStruct(shape, F32) for shape in outs)
    return pl.pallas_call(
        kernel,
        out_shape=outs,
        in_specs=[VMEM] * len(operands),
        out_specs=(VMEM,) * len(outs),
        scratch_shapes=[pltpu.VMEM(shape, F32) for shape in scratch],
        cost_estimate=pl.CostEstimate(flops=flops, bytes_accessed=0, transcendentals=0),
        compiler_params=pltpu.CompilerParams(vmem_limit_bytes=12 * 2**20),
    )(*operands)


def load_kernel(own, rows, copy, rows_copy, part):
    plane = lax.axis_index("group")
    lanes = part.shape[1]
    copy[...] = own[...]
    rows_copy[...] = rows[...]

    @pl.when(plane < 2)
    def _():
        part[...] = rows[:, :lanes]

    @pl.when(plane >= 2)
    def _():
        part[...] = rows[:, lanes // 2 :]


def pair_kernel(own, other, half, even_t, work):
    place = lax.axis_index("tm")
    chip, core = place // 2, lax.rem(place, 2)
    chips, rows, order_dim = half.shape
    used = chip < chips - 1

    def run(even, odd):
        even_t[...] = even[...].T
        for k in range(chips):
            start = pl.multiple_of((2 * k + core) * rows, 8)
            work[k] = even_t[pl.ds(start, rows), :]
        left = parts(work[...].reshape(chips * rows, order_dim))
        half[...] = mul(left, parts(odd[...]), 1).reshape(half.shape)

    pl.when(used & (core == 0))(lambda: run(own, other))
    pl.when(used & (core == 1))(lambda: run(other, own))


def fill(whole, core, mine, theirs):
    whole[:, core] = mine[...]
    whole[:, 1 - core] = theirs[...]


def carry_kernel(even_t, even, step, step_other, skip, skip_other, out, whole):
    place = lax.axis_index("tm")
    chip, core = place // 2, lax.rem(place, 2)
    shape = out.shape

    @pl.when((chip < 2) & (core == 1))
    def _():
        out[...] = even_t[...]

    @pl.when(chip >= 2)
    def _():
        fill(whole, core, step, step_other)
        out[...] = whole[...].reshape(shape)

    @pl.when(chip == 3)
    def _():
        fill(whole, core, skip, skip_other)
        out[...] = mul(parts(whole[...].reshape(shape)), parts(out[...]))

    @pl.when((chip == 2) & (core == 1))
    def _():
        out[...] = mul(parts(out[...]), parts(even_t[...]))

    @pl.when((chip == 3) & (core == 1))
    def _():
        out[...] = mul(parts(out[...]), parts(even[...]), 1)


def local_kernel(rows, beside, skip, cross, carry, out, full):
    place, plane = lax.axis_index("tm"), lax.axis_index("group")
    chip, core = place // 2, lax.rem(place, 2)
    count, lanes = rows.shape[0], skip.shape[1]
    next_to = plane + 1 - 2 * lax.rem(plane, 2)

    def at(block):
        return pl.ds(pl.multiple_of(block * count, 8), count)

    full[at(plane), :] = rows[...]
    full[at(next_to), :] = beside[...]

    @pl.when(plane < 2)
    def _():
        full[at(plane + 2), lanes // 2 :] = skip[...]
        full[at(3 - plane), lanes // 2 :] = cross[...]

    @pl.when(plane >= 2)
    def _():
        full[at(plane - 2), :lanes] = skip[...]
        full[at(3 - plane), :lanes] = cross[...]

    row = lax.broadcasted_iota(jnp.int32, full.shape, 0)
    lane = lax.broadcasted_iota(jnp.int32, full.shape, 1)
    low = (row < 2 * count) & (lane < jnp.where(plane < 2, 2 * lanes, lanes))
    high = (row >= 2 * count) & (lane >= jnp.where(plane < 2, lanes // 2, 0))
    value = jnp.where(low | high, full[...], full[...].T)
    plain = (chip < 2) & (core == 0)

    @pl.when(plain)
    def _():
        out[...] = value

    @pl.when(jnp.logical_not(plain))
    def _():
        left = parts(carry[...])
        out[...] = mul(parts(mul(left, parts(value))), left, 1)


def pick_kernel(first, second, third, out):
    chip = lax.axis_index("tm") // 2
    for k, half in ((1, first), (2, second), (3, third)):

        @pl.when(chip == k)
        def _(half=half):
            out[...] = half[...]


def left_kernel(mine, one, two, out, total):
    place = lax.axis_index("tm")
    chip, core = place // 2, lax.rem(place, 2)
    chips, rows, order_dim = out.shape
    total[...] = one[...] + two[...]

    @pl.when(chip == 0)
    def _():
        for k in range(chips):
            out[k] = total[pl.ds(pl.multiple_of((2 * k + core) * rows, 8), rows), :]

    @pl.when(chip > 0)
    def _():
        left = parts(mine[...].reshape(chips * rows, order_dim))
        out[...] = mul(left, parts(total[...])).reshape(out.shape)


def right_kernel(mine, theirs, left, out, whole):
    place = lax.axis_index("tm")
    chip, core = place // 2, lax.rem(place, 2)
    chips, rows, order_dim = out.shape

    @pl.when(chip == 0)
    def _():
        out[...] = left[...]

    @pl.when(chip > 0)
    def _():
        fill(whole, core, mine, theirs)
        right = parts(whole[...].reshape(order_dim, order_dim))
        out[...] = mul(parts(left[...].reshape(chips * rows, order_dim)), right, 1).reshape(out.shape)


def sum_kernel(terms, *refs):
    received, out = refs[:-1], refs[-1]
    chip = lax.axis_index("tm") // 2
    out[...] = terms[chip] + (received[0][...] + (received[1][...] + received[2][...]))


def body(propagators, perturbation):
    devices = lax.axis_size("tm")
    planes = lax.axis_size("group")
    chips = devices // 2
    order_dim = propagators.shape[1]
    out_rows = order_dim // devices
    chip = lax.axis_index("tm") // 2
    swap = lambda x: lax.ppermute(x, "tm", [(i, i ^ 1) for i in range(devices)])
    cube = 2 * order_dim**3
    block_rows = perturbation.shape[1]
    half_shape = (chips, out_rows, order_dim)
    whole_shape = (chips, 2, out_rows, order_dim)

    own = propagators[0]
    rows = perturbation[0]
    other = swap(own)
    shapes = [own.shape, rows.shape, (block_rows, order_dim // 3 * 2)]
    own, rows, part = call(load_kernel, shapes, [own, rows])
    near = {}
    for name, sent, way in (("beside", rows, 1), ("skip", part, 2), ("cross", part, 3)):
        near[name] = lax.ppermute(sent, "group", [(i, i ^ way) for i in range(planes)])
    half, even_t = call(pair_kernel, [half_shape, own.shape], [own, other], [half_shape], 2 * cube)

    routes = {"skip": [(1, 3)], "step": [(0, 1), (1, 2), (2, 3)], "far": [(0, 3)], "across": [(0, 2)]}
    got, paired = {}, {}
    for name, links in routes.items():
        got[name] = lax.ppermute(half, "tm", [(2 * i + c, 2 * j + c) for i, j in links for c in range(2)])
    for name in ("skip", "step"):
        paired[name] = swap(got[name])
    operands = [even_t, other] + [x[name] for name in ("step", "skip") for x in (got, paired)]
    (carry,) = call(carry_kernel, [own.shape], operands, [whole_shape], 2 * cube)
    operands = [rows] + [near[name] for name in ("beside", "skip", "cross")] + [carry]
    (one,) = call(local_kernel, [own.shape], operands, [own.shape], 6 * cube)
    two = swap(one)
    (mine,) = call(pick_kernel, [half_shape], [got[name] for name in ("step", "across", "far")])
    theirs = swap(mine)
    (left,) = call(left_kernel, [half_shape], [mine, one, two], [own.shape], 2 * cube)
    (terms,) = call(right_kernel, [half_shape], [mine, theirs, left], [whole_shape], 2 * cube)
    received = []
    for way in (3, 2, 1):
        block = lax.dynamic_index_in_dim(terms, chip ^ way, 0, False)
        received.append(lax.ppermute(block, "tm", [(i, i ^ (2 * way)) for i in range(devices)]))
    (out,) = call(sum_kernel, [(out_rows, order_dim)], [terms] + received)
    return out


def plain_body(propagators, perturbation):
    devices = lax.axis_size("tm")
    planes = lax.axis_size("group")
    chips = devices // 2
    order_dim = propagators.shape[1]
    block_rows = perturbation.shape[1]
    out_rows = order_dim // devices
    place = lax.axis_index("tm")
    plane = lax.axis_index("group")
    chip, core = place // 2, place % 2
    partner = [(i, i ^ 1) for i in range(devices)]
    identity = jnp.eye(order_dim, dtype=F32)

    def half_of(whole):
        split = whole.reshape(chips, 2, out_rows, order_dim)
        return lax.dynamic_index_in_dim(split, core, 1, False)

    def by_core(mine, theirs):
        return jnp.where(core == 0, mine, theirs), jnp.where(core == 0, theirs, mine)

    own = propagators[0]
    even, odd = by_core(own, lax.ppermute(own, "tm", partner))
    rows = perturbation[0]
    full = jnp.zeros((order_dim, order_dim), F32)
    for shift in range(planes):
        got = rows
        if shift:
            got = lax.ppermute(rows, "group", [(i, (i + shift) % planes) for i in range(planes)])
        full = lax.dynamic_update_slice_in_dim(full, got, (plane - shift) % planes * block_rows, 0)
    half = half_of(product(even, odd, 0, 1))
    full_even, full_odd = by_core(full, lax.ppermute(full, "tm", partner))
    total = full_even + product(even, product(full_odd, even, 1, 0), 0, 0)
    for shift in range(1, chips):
        got = lax.ppermute(half, "tm", [(i, i + 2 * shift) for i in range(devices - 2 * shift)])
        mine = jnp.where(chip >= shift, got, half_of(identity))
        theirs = lax.ppermute(mine, "tm", partner)
        whole = jnp.stack(by_core(mine, theirs), 1).reshape(order_dim, order_dim)
        total = product(product(whole, total, 1, 0), whole, 1, 1)
    terms = half_of(total)
    out = lax.dynamic_index_in_dim(terms, chip, 0, False)
    for shift in range(1, chips):
        block = lax.dynamic_index_in_dim(terms, (chip + shift) % chips, 0, False)
        out = out + lax.ppermute(block, "tm", [(i, (i + 2 * shift) % devices) for i in range(devices)])
    return out


def solution(mesh):
    in_specs = (P("tm", None, None), P("tm", "group", None))
    out_specs = P("tm", None)
    chips, planes = mesh.shape["tm"] // 2, mesh.shape["group"]

    def step(propagators, perturbation):
        order_dim = propagators.shape[1]
        tiled = order_dim // planes % 8 == 0 and order_dim // (2 * chips) % 8 == 0 and order_dim % 384 == 0
        plan = body if tiled and chips == 4 and planes == 4 else plain_body
        return jax.shard_map(plan, mesh=mesh, in_specs=in_specs, out_specs=out_specs, check_vma=False)(
            propagators, perturbation
        )

    return step
```
